32 devices in a mesh: pb: 4 (over x, core), ka: 4 (over z), ga: 2 (over y).
Axes of the slice: x: 2, y: 2, z: 4, core: 2. Of those that a mesh axis runs over, the one named last changes fastest.
Arguments:
- queries: bfloat16 [16, 512, 768], P(None, 'pb', 'ga'), may hold values from -6 to 6
- comp_keys: bfloat16 [1024, 768], P(('ka', 'pb'), 'ga'), may hold values from -6 to 6
- comp_values: bfloat16 [1024, 512], P(('ka', 'pb'), 'ga'), may hold values from -6 to 6
- outputs: bfloat16 [16, 512, 512], P(None, 'pb', 'ga'), may hold values from -1.1953125 to 1.1953125
- grad_out: bfloat16 [16, 512, 512], P(None, 'pb', 'ga'), may hold values from -300 to 300
- log_sums: float32 [4, 16, 512], P('ga', None, 'pb'), may hold values from 7 to 10
- visible: int32 [8, 1024], P('pb', 'ka'), may hold values from 0 to 1, as said below
Outputs:
- grad_queries: float32 [16, 512, 768], P('ka', 'pb', 'ga')
- grad_keys: float32 [1024, 768], P(('ka', 'pb'), 'ga')
- grad_values: float32 [1024, 512], P(('ka', 'pb'), 'ga')
The draws below stay inside these ranges and needn't reach their ends.
Inputs may be any that keep to these rules, and one draw needn't show every extreme that they name: The queries are the last 512 positions of a sequence of 16384 positions, and compressed key j covers positions 16 * j to 16 * j + 31. visible[b, j] is 1 exactly when key j ends before the first position of query block b and starts no earlier than the start of the document that holds that position; the sequence is packed from a few documents.
All inputs are finite; a program needn't handle non-finite values.
Results may differ from the reference program's by a relative error of at most 0.0029.
Values may be sent and summed in bfloat16 or wider, within the bound.
A program may use at most 64 MiB of HBM per device.

```python
import math
import jax
import jax.numpy as jnp
from jax import lax

G = 4
HG = 16
DK = 192
DV = 128
QBLK = 64
STRIDE = 16
SPAN = 32
NQ = 512
KEYS = 1024
NQB = 8


def draw_visible(key, part):
    positions = KEYS * STRIDE
    starts = jax.random.randint(jax.random.fold_in(key, 11), (2,), 0, positions)
    window_start = positions - NQB * QBLK
    block_first = window_start + jnp.arange(NQB, dtype=jnp.int32) * QBLK
    key_first = jnp.arange(KEYS, dtype=jnp.int32) * STRIDE
    key_last = key_first + SPAN - 1
    doc_start = jnp.max(jnp.where(starts[None, :] <= block_first[:, None], starts[None, :], 0), axis=1)
    drawn = (key_last[None, :] < block_first[:, None]) & (key_first[None, :] >= doc_start[:, None])
    return drawn.astype(jnp.int32)


def block_scale(key, dims, pieces, smallest, high):
    def one(dim, blocks):
        heights = jax.random.uniform(jax.random.fold_in(jax.random.fold_in(key, 6), dim), (blocks,), jnp.float32, smallest / len(pieces), high / len(pieces))
        return jnp.repeat(jnp.exp(heights), dims[dim] // blocks).reshape((-1,) + (1,) * (len(dims) - dim - 1))

    level = one(*pieces[0])
    for cut in pieces[1:]:
        level = level * one(*cut)
    return level


def scatter_about(own_key, shape, spread, bound, pieces=(), kind=jnp.bfloat16):
    entries = spread * jax.random.normal(own_key, shape, jnp.float32)
    if pieces:
        entries = entries * block_scale(own_key, shape, pieces, -0.22, 0.18)
    return jnp.clip(entries, -bound, bound).astype(kind)


def setup_inputs(seed: int = 0) -> dict:
    key_list = jax.random.split(jax.random.key(seed), 8)
    queries = scatter_about(key_list[0], (HG, NQ, G * DK), 1.0, 6.0, ((1, 4), (2, 2)))
    comp_keys = scatter_about(key_list[1], (KEYS, G * DK), 1.0, 6.0, ((0, 16), (1, 2)))
    comp_values = scatter_about(key_list[2], (KEYS, G * DV), 1.0, 6.0, ((0, 16), (1, 2)))
    outputs = scatter_about(key_list[3], (HG, NQ, G * DV), 0.2, 1.1953125, ((1, 4), (2, 2)))
    grad_out = scatter_about(key_list[4], (HG, NQ, G * DV), 50.0, 300.0, ((1, 4), (2, 2)))
    log_sums = jnp.clip(7.0 + 3.0 * jax.random.uniform(key_list[5], (G, HG, NQ), jnp.float32) ** block_scale(key_list[5], (G, HG, NQ), ((0, 2), (2, 4)), -0.2, 0.2), 7.0, 10.0)
    visible = draw_visible(jax.random.fold_in(key_list[7], 71), 0)
    return dict(queries=queries, comp_keys=comp_keys, comp_values=comp_values, outputs=outputs, grad_out=grad_out, log_sums=log_sums, visible=visible)


def reference(queries, comp_keys, comp_values, outputs, grad_out, log_sums, visible):
    softmax_scale = 1.0 / math.sqrt(DK)
    block_rows = min(512, KEYS)
    blocks = KEYS // block_rows
    query_total = queries.shape[1]
    mask_blocks = visible.reshape(NQB, blocks, block_rows).transpose(1, 0, 2)
    grads_query = []
    grads_key = []
    grads_value = []
    for group_index in range(G):
        query_group = queries[:, :, group_index * DK:(group_index + 1) * DK].astype(jnp.float32)
        grad_group = grad_out[:, :, group_index * DV:(group_index + 1) * DV].astype(jnp.float32)
        out_group = outputs[:, :, group_index * DV:(group_index + 1) * DV].astype(jnp.float32)
        row_delta = lax.optimization_barrier(jnp.sum(grad_group * out_group, axis=2))
        row_lse = log_sums[group_index]
        key_group = comp_keys[:, group_index * DK:(group_index + 1) * DK].reshape(blocks, block_rows, DK)
        value_group = comp_values[:, group_index * DV:(group_index + 1) * DV].reshape(blocks, block_rows, DV)

        def advance(running, inputs, query_group=query_group, grad_group=grad_group, row_delta=row_delta, row_lse=row_lse):
            key_block, value_block, mask_block = inputs
            key_float = key_block.astype(jnp.float32)
            scores = jnp.einsum('hqd,kd->hqk', query_group, key_float) * softmax_scale
            weights = jnp.repeat(mask_block, QBLK, axis=0).astype(jnp.float32)
            probs_full = jnp.exp(scores - row_lse[:, :, None]) * weights[None]
            probs_low = lax.optimization_barrier(probs_full.astype(jnp.bfloat16)).astype(jnp.float32)
            grad_probs = jnp.einsum('hqd,kd->hqk', grad_group, value_block.astype(jnp.float32))
            grad_scores = probs_full * (grad_probs - row_delta[:, :, None])
            grad_low = lax.optimization_barrier(grad_scores.astype(jnp.bfloat16)).astype(jnp.float32)
            value_grad = jnp.einsum('hqk,hqd->kd', probs_low, grad_group)
            key_grad = jnp.einsum('hqk,hqd->kd', grad_low, query_group) * softmax_scale
            query_grad = jnp.einsum('hqk,kd->hqd', grad_low, key_float) * softmax_scale
            return (running + query_grad, (key_grad, value_grad))
        initial = jnp.zeros((HG, query_total, DK), jnp.float32)
        query_sum, (key_parts, value_parts) = lax.scan(advance, initial, (key_group, value_group, mask_blocks))
        grads_query.append(query_sum)
        grads_key.append(key_parts.reshape(KEYS, DK))
        grads_value.append(value_parts.reshape(KEYS, DV))
    return (jnp.concatenate(grads_query, axis=2), jnp.concatenate(grads_key, axis=1), jnp.concatenate(grads_value, axis=1))
```

```python
import functools

import jax
import jax.numpy as jnp
from jax import lax
from jax.experimental import pallas as pl
from jax.experimental.pallas import tpu as pltpu
from jax.sharding import PartitionSpec as P

DK = 192
DV = 128
LANES = 128
MESH = pl.DeviceIdType.MESH


def flip(index, bits):
    bit = 1
    while bit <= bits:
        if bits & bit:
            index = index + bit - 2 * bit * ((index // bit) % 2)
        bit *= 2
    return index


def low_bit(m):
    return m & -m


def window(group):
    start = group * DK // LANES * LANES
    stop = -(-(group + 1) * DK // LANES) * LANES
    return start, stop


def keep_group(block, group):
    start, stop = window(group)
    lane = lax.broadcasted_iota(jnp.int32, block.shape, 1) + start
    inside = (lane >= group * DK) & (lane < (group + 1) * DK)
    return jnp.where(inside, block, jnp.zeros_like(block))


def dot(a, b, ca, cb):
    return lax.dot_general(a, b, (((ca,), (cb,)), ((), ())), preferred_element_type=jnp.float32)


def kernel(n_pb, n_ka, groups, heads, nq, rows, n_blocks, *refs):
    bits = n_pb.bit_length() - 1
    q_hbm, k_hbm, v_hbm, o_hbm, do_hbm, lse_hbm, vis_hbm = refs[:7]
    dq_ref, dk_ref, dv_ref = refs[7:10]
    (kv, qv, dov, ov, lse, vis, qm, stat, dq_acc, acc) = refs[10:20]
    rest = list(refs[20:])
    recvs = [rest.pop(0) for _ in range(bits)]
    sends = [None] + [rest.pop(0) for _ in range(bits - 1)]
    zs, zr, loc_sem, ag_s, ag_r, vs_s, vs_r, rs_s, rs_r, z_s, z_r = rest

    ka = lax.axis_index("ka")
    pb = lax.axis_index("pb")
    scale = DK ** (-0.5)
    dk_cols = groups * DK
    keys_ka = n_pb * rows
    hq = heads * nq

    locals_ = [
        (k_hbm, kv.at[ka, pb, :, pl.ds(0, dk_cols)]),
        (v_hbm, kv.at[ka, pb, :, pl.ds(dk_cols, groups * DV)]),
        (vis_hbm, vis.at[ka]),
        (q_hbm.at[pl.ds(ka * heads, heads)], qv),
        (do_hbm.at[pl.ds(ka * heads, heads)], dov),
        (o_hbm.at[pl.ds(ka * heads, heads)], ov),
        (lse_hbm, lse),
    ]
    loc = [pltpu.make_async_copy(a, b, loc_sem.at[i]) for i, (a, b) in enumerate(locals_)]
    for c in loc:
        c.start()

    barrier = pltpu.get_barrier_semaphore()
    for j in range(1, n_ka):
        pl.semaphore_signal(barrier, inc=1, device_id={"ka": flip(ka, j)}, device_id_type=MESH)
    for t in range(bits):
        pl.semaphore_signal(barrier, inc=1, device_id={"pb": flip(pb, 1 << t)}, device_id_type=MESH)
    for c in loc[:3]:
        c.wait()
    pl.semaphore_wait(barrier, n_ka - 1 + bits)

    pending = []

    def remote(src, dst, s_sem, r_sem, **peer):
        return pltpu.make_async_remote_copy(
            src_ref=src, dst_ref=dst, send_sem=s_sem, recv_sem=r_sem,
            device_id=peer, device_id_type=MESH,
        )

    def send(*args, **peer):
        copy = remote(*args, **peer)
        copy.start()
        pending.append(copy)

    def shard(j, m):
        return kv.at[flip(ka, j), flip(pb, m)]

    def wait_shard(j, m):
        peer = {"pb": flip(pb, low_bit(m))} if m else {"ka": flip(ka, j)}
        remote(shard(j, m), shard(j, m), ag_s.at[j, m], ag_r.at[j, m], **peer).wait_recv()

    def forward(j, m):
        bit = n_pb // 2
        while bit:
            if m == 0 or bit < low_bit(m):
                send(shard(j, m), shard(j, m), ag_s.at[j, m ^ bit], ag_r.at[j, m ^ bit], pb=flip(pb, bit))
            bit //= 2

    def relay(j):
        if j:
            wait_shard(j, 0)
            forward(j, 0)
        bit = n_pb // 2
        while bit > 1:
            for m in range(bit, n_pb, 2 * bit):
                wait_shard(j, m)
                forward(j, m)
            bit //= 2

    for j in range(1, n_ka):
        send(kv.at[ka, pb], kv.at[ka, pb], ag_s.at[j, 0], ag_r.at[j, 0], ka=flip(ka, j))
    forward(0, 0)
    for j in range(1, n_ka):
        send(vis.at[ka], vis.at[ka], vs_s.at[j], vs_r.at[j], ka=flip(ka, j))

    for c in loc[3:]:
        c.wait()
    for g in range(groups):
        start, stop = window(g)
        qm[g] = keep_group(qv[:, :, start:stop].reshape(hq, stop - start), g)
        product = dov[:, :, g * DV : (g + 1) * DV].astype(jnp.float32) * ov[
            :, :, g * DV : (g + 1) * DV
        ].astype(jnp.float32)
        row_delta = jnp.sum(jnp.transpose(product.reshape(hq, DV)), axis=0, keepdims=True)
        stat[2 * g + 1 : 2 * g + 2, :] = row_delta
        for h in range(heads):
            stat[2 * g : 2 * g + 1, h * nq : (h + 1) * nq] = lse[g, pl.ds(ka * heads + h, 1), :]

    per = min(n_pb, max(1, 256 // rows))
    chunk_rows = per * rows

    def compute_chunk(j, chunk):
        s = flip(ka, j)
        whole = kv[s, pl.ds(chunk * per, per)].reshape(chunk_rows, dk_cols + groups * DV)
        if per == n_pb:
            seen = vis[s]
        else:
            seen = vis[s, :, pl.ds(pl.multiple_of(chunk * chunk_rows, chunk_rows), chunk_rows)]
        seen = seen.astype(jnp.float32)
        block = lax.broadcasted_iota(jnp.int32, (nq, chunk_rows), 0) // (nq // n_blocks)
        mask = jnp.zeros((nq, chunk_rows), jnp.float32)
        for b in range(n_blocks):
            mask = jnp.where(block == b, seen[b : b + 1, :], mask)
        mask = jnp.transpose(mask)
        mask = jnp.concatenate([mask] * heads, axis=1)
        tiles = {}
        for g in range(groups):
            start, stop = window(g)
            keys = keep_group(whole[:, start:stop], g)
            values = whole[:, dk_cols + g * DV : dk_cols + (g + 1) * DV]
            grad = dov[:, :, g * DV : (g + 1) * DV].reshape(hq, DV)
            query = qm[g]
            scores = dot(keys, query, 1, 1) * scale
            probs = jnp.exp(scores - stat[2 * g : 2 * g + 1, :]) * mask
            grad_probs = dot(values, grad, 1, 1)
            grad_scores = (probs * (grad_probs - stat[2 * g + 1 : 2 * g + 2, :])).astype(jnp.bfloat16)
            value_grad = dot(probs.astype(jnp.bfloat16), grad, 1, 0)
            acc[j, pl.ds(chunk * per, per), :, dk_cols + g * DV : dk_cols + (g + 1) * DV] = (
                value_grad.reshape(per, rows, DV)
            )
            key_grad = dot(grad_scores, query, 1, 0)
            for c in range(start, stop, LANES):
                part = key_grad[:, c - start : c - start + LANES]
                tiles[c] = tiles[c] + part if c in tiles else part
            query_grad = dot(grad_scores, keys, 0, 0)
            dq_acc[:, start:stop] += query_grad
        for c, tile in tiles.items():
            acc[j, pl.ds(chunk * per, per), :, c : c + LANES] = tile.reshape(per, rows, LANES)

    def compute(j):
        for m in range(1, n_pb, 2):
            wait_shard(j, m)
        if j:
            s = flip(ka, j)
            remote(vis.at[s], vis.at[s], vs_s.at[j], vs_r.at[j], ka=s).wait_recv()
        if per == n_pb:
            compute_chunk(j, 0)
        else:
            lax.fori_loop(0, n_pb // per, lambda c, _: (compute_chunk(j, c), 0)[1], 0)
        for m in range(1, n_pb, 2):
            send(acc.at[j, flip(pb, m)], recvs[0].at[j, m >> 1], rs_s.at[j, m], rs_r.at[j, m], pb=flip(pb, 1))

    def reduce_stage(j, t):
        step = 2 << t
        for m in range(0, n_pb, step):
            slot = recvs[t].at[j, m >> (t + 1)]
            sem = m + (1 << t)
            remote(slot, slot, rs_s.at[j, sem], rs_r.at[j, sem], pb=flip(pb, 1 << t)).wait_recv()
            mine = flip(pb, m)
            total = acc[j, mine] + slot[...].astype(jnp.float32)
            if m & step:
                at = m >> (t + 2)
                sends[t + 1][j, at] = total.astype(jnp.bfloat16)
                send(
                    sends[t + 1].at[j, at], recvs[t + 1].at[j, at],
                    rs_s.at[j, m], rs_r.at[j, m], pb=flip(pb, step),
                )
            elif t == bits - 1 and j:
                zs[j] = total.astype(jnp.bfloat16)
                send(zs.at[j], zr.at[j], z_s.at[j], z_r.at[j], ka=flip(ka, j))
            else:
                acc[j, mine] = total

    dq_acc[...] = jnp.zeros_like(dq_acc)
    relay(0)
    relay(min(1, n_ka - 1))
    for i in range(n_ka + bits):
        if i < n_ka:
            compute(i)
        if i + 2 < n_ka:
            relay(i + 2)
        for t in range(bits - 1, -1, -1):
            if 0 <= i - 1 - t < n_ka:
                reduce_stage(i - 1 - t, t)
        if i == n_ka - 1:
            for h in range(heads):
                dq_ref[h] = dq_acc[h * nq : (h + 1) * nq, :] * scale

    total = acc[0, pb]
    for j in range(1, n_ka):
        remote(zr.at[j], zr.at[j], z_s.at[j], z_r.at[j], ka=flip(ka, j)).wait_recv()
        total = total + zr[j].astype(jnp.float32)
    dk_ref[...] = total[:, :dk_cols] * scale
    dv_ref[...] = total[:, dk_cols:]
    for copy in pending:
        copy.wait_send()


def per_device(n_pb, n_ka, queries, comp_keys, comp_values, outputs, grad_out, log_sums, visible):
    groups = comp_keys.shape[1] // DK
    all_heads, nq, _ = queries.shape
    heads = all_heads // n_ka
    rows = comp_keys.shape[0]
    cols = comp_keys.shape[1] + comp_values.shape[1]
    bits = n_pb.bit_length() - 1
    n_blocks = visible.shape[0]
    f32, bf16 = jnp.float32, jnp.bfloat16
    width = window(0)[1] - window(0)[0]
    hq = heads * nq
    scratch = [
        pltpu.VMEM((n_ka, n_pb, rows, cols), bf16),
        pltpu.VMEM((heads, nq, queries.shape[2]), bf16),
        pltpu.VMEM((heads, nq, grad_out.shape[2]), bf16),
        pltpu.VMEM((heads, nq, grad_out.shape[2]), bf16),
        pltpu.VMEM(log_sums.shape, f32),
        pltpu.VMEM((n_ka,) + visible.shape, jnp.int32),
        pltpu.VMEM((groups, hq, width), bf16),
        pltpu.VMEM((2 * groups, hq), f32),
        pltpu.VMEM((hq, groups * DK), f32),
        pltpu.VMEM((n_ka, n_pb, rows, cols), f32),
    ]
    scratch += [
        pltpu.VMEM((n_ka, n_pb >> (t + 1), rows, cols), f32 if t == 0 else bf16) for t in range(bits)
    ]
    scratch += [pltpu.VMEM((n_ka, n_pb >> (t + 1), rows, cols), bf16) for t in range(1, bits)]
    dma = pltpu.SemaphoreType.DMA
    scratch += [
        pltpu.VMEM((n_ka, rows, cols), bf16),
        pltpu.VMEM((n_ka, rows, cols), bf16),
        dma((7,)),
        dma((n_ka, n_pb)),
        dma((n_ka, n_pb)),
        dma((n_ka,)),
        dma((n_ka,)),
        dma((n_ka, n_pb)),
        dma((n_ka, n_pb)),
        dma((n_ka,)),
        dma((n_ka,)),
    ]
    return pl.pallas_call(
        functools.partial(kernel, n_pb, n_ka, groups, heads, nq, rows, n_blocks),
        out_shape=(
            jax.ShapeDtypeStruct((heads, nq, queries.shape[2]), f32),
            jax.ShapeDtypeStruct(comp_keys.shape, f32),
            jax.ShapeDtypeStruct(comp_values.shape, f32),
        ),
        in_specs=[pl.BlockSpec(memory_space=pl.ANY)] * 7,
        out_specs=[pl.BlockSpec(memory_space=pltpu.VMEM)] * 3,
        scratch_shapes=scratch,
        compiler_params=pltpu.CompilerParams(
            collective_id=0, has_side_effects=True, vmem_limit_bytes=64000 * 1024
        ),
    )(queries, comp_keys, comp_values, outputs, grad_out, log_sums, visible)


def solution(mesh):
    n_pb, n_ka = mesh.shape["pb"], mesh.shape["ka"]
    return jax.shard_map(
        functools.partial(per_device, n_pb, n_ka),
        mesh=mesh,
        in_specs=(
            P(None, "pb", "ga"),
            P(("ka", "pb"), "ga"),
            P(("ka", "pb"), "ga"),
            P(None, "pb", "ga"),
            P(None, "pb", "ga"),
            P("ga", None, "pb"),
            P("pb", "ka"),
        ),
        out_specs=(P("ka", "pb", "ga"), P(("ka", "pb"), "ga"), P(("ka", "pb"), "ga")),
        check_vma=False,
    )
```

```python
import functools

import jax
import jax.numpy as jnp
from jax import lax
from jax.experimental import pallas as pl
from jax.experimental.pallas import tpu as pltpu
from jax.sharding import PartitionSpec as P

DK = 192
DV = 128
LANES = 128
MESH = pl.DeviceIdType.MESH


def flip(index, bits):
    bit = 1
    while bit <= bits:
        if bits & bit:
            index = index + bit - 2 * bit * ((index // bit) % 2)
        bit *= 2
    return index


def low_bit(m):
    return m & -m


def tile_start(group):
    return group * DK // LANES * LANES


def keep_group(block, group):
    axis = block.ndim - 1
    lane = lax.broadcasted_iota(jnp.int32, block.shape, axis) + tile_start(group)
    inside = (lane >= group * DK) & (lane < (group + 1) * DK)
    return jnp.where(inside, block, jnp.zeros_like(block))


def half_roll(block):
    return pltpu.roll(block, LANES // 2, block.ndim - 1)


def pack(block, group):
    first, second = block[..., :LANES], block[..., LANES:]
    even = group % 2 == 0
    full = jnp.where(even, first, second)
    half = jnp.where(even, second, first)
    rows = block.shape[1] // 2
    return full, half[:, :rows] + half_roll(half[:, rows:])


def unpack(full, folded, group):
    even = group % 2 == 0
    lane = lax.broadcasted_iota(jnp.int32, folded.shape, 2)
    inside = (lane < LANES // 2) == even
    low = jnp.where(inside, folded, 0.0)
    high = jnp.where(inside, half_roll(folded), 0.0)
    half = jnp.concatenate([low, high], axis=1)
    return jnp.where(even, full, half), jnp.where(even, half, full)


def dot(a, b, ca, cb):
    return lax.dot_general(a, b, (((ca,), (cb,)), ((), ())), preferred_element_type=jnp.float32)


def kernel(n_pb, n_ka, groups, own_heads, nq, rows, n_blocks, *refs):
    bits = n_pb.bit_length() - 1
    q_hbm, k_hbm, v_hbm, o_hbm, do_hbm, lse_hbm, vis_hbm = refs[:7]
    dq_ref, dk_ref, dv_ref = refs[7:10]
    (kv, own, qv, dov, ov, lse, vis, stat, dq_acc, dq_full, dq_s, dq_r, acc, whole_grad) = refs[10:24]
    rest = list(refs[24:])
    recvs = [rest.pop(0) for _ in range(bits)]
    sends = [None] + [rest.pop(0) for _ in range(bits - 1)]
    zs, zr, loc_sem, ag_s, ag_r, vs_s, vs_r, rs_s, rs_r, z_s, z_r, q_s, q_r = rest

    ka = lax.axis_index("ka")
    pb = lax.axis_index("pb")
    scale = DK ** (-0.5)
    width = 2 * LANES
    heads = own_heads * groups
    group = ka % groups
    first_head = (ka // groups) * heads
    hq = heads * nq
    k_start = pl.multiple_of(tile_start(group), LANES)
    v_start = pl.multiple_of(group * DV, LANES)
    head_part = pl.ds(first_head, heads)

    locals_ = [
        (k_hbm.at[:, pl.ds(k_start, width)], kv.at[ka, pb, :, pl.ds(0, width)]),
        (v_hbm.at[:, pl.ds(v_start, DV)], kv.at[ka, pb, :, pl.ds(width, DV)]),
    ]
    for g in range(groups):
        locals_ += [
            (k_hbm.at[:, pl.ds(tile_start(g), width)], own.at[g, :, pl.ds(0, width)]),
            (v_hbm.at[:, pl.ds(g * DV, DV)], own.at[g, :, pl.ds(width, DV)]),
        ]
    locals_ += [(vis_hbm, vis.at[ka])]
    first = len(locals_)
    locals_ += [
        (q_hbm.at[head_part, :, pl.ds(k_start, width)], qv),
        (do_hbm.at[head_part, :, pl.ds(v_start, DV)], dov),
        (o_hbm.at[head_part, :, pl.ds(v_start, DV)], ov),
        (lse_hbm, lse),
    ]
    loc = [pltpu.make_async_copy(a, b, loc_sem.at[i]) for i, (a, b) in enumerate(locals_)]
    for c in loc:
        c.start()

    barrier = pltpu.get_barrier_semaphore()
    for j in range(1, n_ka):
        pl.semaphore_signal(barrier, inc=1, device_id={"ka": flip(ka, j)}, device_id_type=MESH)
    for t in range(bits):
        pl.semaphore_signal(barrier, inc=1, device_id={"pb": flip(pb, 1 << t)}, device_id_type=MESH)
    for c in loc[:first]:
        c.wait()
    pl.semaphore_wait(barrier, n_ka - 1 + bits)

    pending = []

    def remote(src, dst, s_sem, r_sem, **peer):
        return pltpu.make_async_remote_copy(
            src_ref=src, dst_ref=dst, send_sem=s_sem, recv_sem=r_sem,
            device_id=peer, device_id_type=MESH,
        )

    def send(*args, **peer):
        copy = remote(*args, **peer)
        copy.start()
        pending.append(copy)

    def shard(j, m):
        return kv.at[flip(ka, j), flip(pb, m)]

    def wait_shard(j, m):
        peer = {"pb": flip(pb, low_bit(m))} if m else {"ka": flip(ka, j)}
        remote(shard(j, m), shard(j, m), ag_s.at[j, m], ag_r.at[j, m], **peer).wait_recv()

    def forward(j, m):
        bit = n_pb // 2
        while bit:
            if m == 0 or bit < low_bit(m):
                send(shard(j, m), shard(j, m), ag_s.at[j, m ^ bit], ag_r.at[j, m ^ bit], pb=flip(pb, bit))
            bit //= 2

    def relay(j):
        if j:
            wait_shard(j, 0)
            forward(j, 0)
        bit = n_pb // 2
        while bit > 1:
            for m in range(bit, n_pb, 2 * bit):
                wait_shard(j, m)
                forward(j, m)
            bit //= 2

    for j in range(1, n_ka):
        far = flip(ka, j)
        send(own.at[far % groups], kv.at[ka, pb], ag_s.at[j, 0], ag_r.at[j, 0], ka=far)
    forward(0, 0)
    for j in range(1, n_ka):
        send(vis.at[ka], vis.at[ka], vs_s.at[j], vs_r.at[j], ka=flip(ka, j))

    for c in loc[first:]:
        c.wait()
    qv[...] = keep_group(qv[...], group)
    product = dov[...].astype(jnp.float32) * ov[...].astype(jnp.float32)
    stat[1:2, :] = jnp.sum(jnp.transpose(product.reshape(hq, DV)), axis=0, keepdims=True)
    for h in range(heads):
        stat[0:1, h * nq : (h + 1) * nq] = lse[group, pl.ds(first_head + h, 1), :]
    dq_acc[...] = jnp.zeros_like(dq_acc)

    per = min(n_pb, max(1, 256 // rows))
    chunk_rows = per * rows

    def compute_chunk(j, chunk):
        s = flip(ka, j)
        whole = kv[s, pl.ds(chunk * per, per)].reshape(chunk_rows, width + DV)
        if per == n_pb:
            seen = vis[s]
        else:
            seen = vis[s, :, pl.ds(pl.multiple_of(chunk * chunk_rows, chunk_rows), chunk_rows)]
        seen = seen.astype(jnp.float32)
        block = lax.broadcasted_iota(jnp.int32, (nq, chunk_rows), 0) // (nq // n_blocks)
        mask = jnp.zeros((nq, chunk_rows), jnp.float32)
        for b in range(n_blocks):
            mask = jnp.where(block == b, seen[b : b + 1, :], mask)
        mask = jnp.transpose(mask)
        mask = jnp.concatenate([mask] * heads, axis=1)
        keys = keep_group(whole[:, :width], group)
        values = whole[:, width:]
        grad = dov[...].reshape(hq, DV)
        query = qv[...].reshape(hq, width)
        scores = dot(keys, query, 1, 1) * scale
        probs = jnp.exp(scores - stat[0:1, :]) * mask
        grad_probs = dot(values, grad, 1, 1)
        grad_scores = (probs * (grad_probs - stat[1:2, :])).astype(jnp.bfloat16)
        value_grad = dot(probs.astype(jnp.bfloat16), grad, 1, 0)
        at = pl.ds(chunk * per, per)
        acc[j, at, 0:rows] = value_grad.reshape(per, rows, DV)
        key_grad = dot(grad_scores, query, 1, 0)
        full, folded = pack(key_grad.reshape(per, rows, width), group)
        acc[j, at, rows : 2 * rows] = full
        acc[j, at, 2 * rows :] = folded
        dq_acc[...] += dot(grad_scores, keys, 0, 0)

    def compute(j):
        for m in range(1, n_pb, 2):
            wait_shard(j, m)
        if j:
            s = flip(ka, j)
            remote(vis.at[s], vis.at[s], vs_s.at[j], vs_r.at[j], ka=s).wait_recv()
        if per == n_pb:
            compute_chunk(j, 0)
        else:
            lax.fori_loop(0, n_pb // per, lambda c, _: (compute_chunk(j, c), 0)[1], 0)
        for m in range(1, n_pb, 2):
            send(acc.at[j, flip(pb, m)], recvs[0].at[j, m >> 1], rs_s.at[j, m], rs_r.at[j, m], pb=flip(pb, 1))

    def reduce_stage(j, t):
        step = 2 << t
        for m in range(0, n_pb, step):
            slot = recvs[t].at[j, m >> (t + 1)]
            sem = m + (1 << t)
            remote(slot, slot, rs_s.at[j, sem], rs_r.at[j, sem], pb=flip(pb, 1 << t)).wait_recv()
            mine = flip(pb, m)
            total = acc[j, mine] + slot[...].astype(jnp.float32)
            if m & step:
                at = m >> (t + 2)
                sends[t + 1][j, at] = total.astype(jnp.bfloat16)
                send(
                    sends[t + 1].at[j, at], recvs[t + 1].at[j, at],
                    rs_s.at[j, m], rs_r.at[j, m], pb=flip(pb, step),
                )
            elif t == bits - 1 and j:
                zs[j] = total.astype(jnp.bfloat16)
                send(zs.at[j], zr.at[j], z_s.at[j], z_r.at[j], ka=flip(ka, j))
            else:
                acc[j, mine] = total

    def send_queries():
        for r in range(1, groups):
            far = flip(ka, r)
            part = dq_acc[pl.ds(pl.multiple_of((far % groups) * own_heads * nq, nq), own_heads * nq), :]
            full, folded = pack(part.reshape(own_heads, nq, width), group)
            dq_s[r, :, :nq] = full.astype(jnp.bfloat16)
            dq_s[r, :, nq:] = folded.astype(jnp.bfloat16)
            send(dq_s.at[r], dq_r.at[r], q_s.at[r], q_r.at[r], ka=far)
        mine = dq_acc[pl.ds(pl.multiple_of(group * own_heads * nq, nq), own_heads * nq), :]
        dq_full[group] = mine.reshape(own_heads, nq, width)

    relay(0)
    relay(min(1, n_ka - 1))
    for i in range(n_ka + bits):
        if i < n_ka:
            compute(i)
        if i + 2 < n_ka:
            relay(i + 2)
        if i == n_ka - 1:
            send_queries()
        for t in range(bits - 1, -1, -1):
            if 0 <= i - 1 - t < n_ka:
                reduce_stage(i - 1 - t, t)

    def join(pieces, columns):
        tiles = {}
        for g in range(groups):
            for c in range(2):
                at = tile_start(g) + c * LANES
                tile = pieces[g][c]
                tiles[at] = tiles[at] + tile if at in tiles else tile
        return [(at, tile) for at, tile in tiles.items() if at < columns]

    for r in range(1, groups):
        far = flip(ka, r)
        remote(dq_r.at[r], dq_r.at[r], q_s.at[r], q_r.at[r], ka=far).wait_recv()
        got = dq_r[r].astype(jnp.float32)
        left, right = unpack(got[:, :nq], got[:, nq:], far % groups)
        dq_full[far % groups, :, :, :LANES] = left
        dq_full[far % groups, :, :, LANES:] = right
    pieces = [(dq_full[g, :, :, :LANES], dq_full[g, :, :, LANES:]) for g in range(groups)]
    for at, tile in join(pieces, groups * DK):
        dq_ref[:, :, at : at + LANES] = tile * scale

    totals = [acc[0, pb]] + [None] * (groups - 1)
    for j in range(1, n_ka):
        remote(zr.at[j], zr.at[j], z_s.at[j], z_r.at[j], ka=flip(ka, j)).wait_recv()
        term = zr[j].astype(jnp.float32)
        r = j % groups
        totals[r] = term if totals[r] is None else totals[r] + term
    for r in range(groups):
        whole_grad[flip(group, r)] = totals[r]
    pieces = []
    for g in range(groups):
        dv_ref[:, g * DV : (g + 1) * DV] = whole_grad[g, 0:rows]
        left, right = unpack(
            whole_grad[g, rows : 2 * rows][None], whole_grad[g, 2 * rows :][None], jnp.int32(g)
        )
        pieces.append((left[0], right[0]))
    for at, tile in join(pieces, groups * DK):
        dk_ref[:, at : at + LANES] = tile * scale
    for copy in pending:
        copy.wait_send()


def per_device(n_pb, n_ka, queries, comp_keys, comp_values, outputs, grad_out, log_sums, visible):
    groups = comp_keys.shape[1] // DK
    all_heads, nq, _ = queries.shape
    heads = all_heads // n_ka
    rows = comp_keys.shape[0]
    bits = n_pb.bit_length() - 1
    n_blocks = visible.shape[0]
    f32, bf16 = jnp.float32, jnp.bfloat16
    width = 2 * LANES
    team = heads * groups
    packed = 2 * rows + rows // 2
    scratch = [
        pltpu.VMEM((n_ka, n_pb, rows, width + DV), bf16),
        pltpu.VMEM((groups, rows, width + DV), bf16),
        pltpu.VMEM((team, nq, width), bf16),
        pltpu.VMEM((team, nq, DV), bf16),
        pltpu.VMEM((team, nq, DV), bf16),
        pltpu.VMEM(log_sums.shape, f32),
        pltpu.VMEM((n_ka,) + visible.shape, jnp.int32),
        pltpu.VMEM((2, team * nq), f32),
        pltpu.VMEM((team * nq, width), f32),
        pltpu.VMEM((groups, heads, nq, width), f32),
        pltpu.VMEM((groups, heads, nq + nq // 2, LANES), bf16),
        pltpu.VMEM((groups, heads, nq + nq // 2, LANES), bf16),
        pltpu.VMEM((n_ka, n_pb, packed, LANES), f32),
        pltpu.VMEM((groups, packed, LANES), f32),
    ]
    scratch += [
        pltpu.VMEM((n_ka, n_pb >> (t + 1), packed, LANES), f32 if t == 0 else bf16)
        for t in range(bits)
    ]
    scratch += [pltpu.VMEM((n_ka, n_pb >> (t + 1), packed, LANES), bf16) for t in range(1, bits)]
    dma = pltpu.SemaphoreType.DMA
    scratch += [
        pltpu.VMEM((n_ka, packed, LANES), bf16),
        pltpu.VMEM((n_ka, packed, LANES), bf16),
        dma((7 + 2 * groups,)),
        dma((n_ka, n_pb)),
        dma((n_ka, n_pb)),
        dma((n_ka,)),
        dma((n_ka,)),
        dma((n_ka, n_pb)),
        dma((n_ka, n_pb)),
        dma((n_ka,)),
        dma((n_ka,)),
        dma((groups,)),
        dma((groups,)),
    ]
    return pl.pallas_call(
        functools.partial(kernel, n_pb, n_ka, groups, heads, nq, rows, n_blocks),
        out_shape=(
            jax.ShapeDtypeStruct((heads, nq, queries.shape[2]), f32),
            jax.ShapeDtypeStruct(comp_keys.shape, f32),
            jax.ShapeDtypeStruct(comp_values.shape, f32),
        ),
        in_specs=[pl.BlockSpec(memory_space=pl.ANY)] * 7,
        out_specs=[pl.BlockSpec(memory_space=pltpu.VMEM)] * 3,
        scratch_shapes=scratch,
        compiler_params=pltpu.CompilerParams(
            collective_id=0, has_side_effects=True, vmem_limit_bytes=64000 * 1024
        ),
    )(queries, comp_keys, comp_values, outputs, grad_out, log_sums, visible)


def solution(mesh):
    n_pb, n_ka = mesh.shape["pb"], mesh.shape["ka"]
    return jax.shard_map(
        functools.partial(per_device, n_pb, n_ka),
        mesh=mesh,
        in_specs=(
            P(None, "pb", "ga"),
            P(("ka", "pb"), "ga"),
            P(("ka", "pb"), "ga"),
            P(None, "pb", "ga"),
            P(None, "pb", "ga"),
            P("ga", None, "pb"),
            P("pb", "ka"),
        ),
        out_specs=(P("ka", "pb", "ga"), P(("ka", "pb"), "ga"), P(("ka", "pb"), "ga")),
        check_vma=False,
    )
```

```python
import functools

import jax
import jax.numpy as jnp
from jax import lax
from jax.experimental import pallas as pl
from jax.experimental.pallas import tpu as pltpu
from jax.sharding import PartitionSpec as P

DK = 192
DV = 128
LANES = 128
MESH = pl.DeviceIdType.MESH


def flip(index, bits):
    bit = 1
    while bit <= bits:
        if bits & bit:
            index = index + bit - 2 * bit * ((index // bit) % 2)
        bit *= 2
    return index


def low_bit(m):
    return m & -m


def tile_start(group):
    return group * DK // LANES * LANES


def keep_group(block, group):
    axis = block.ndim - 1
    lane = lax.broadcasted_iota(jnp.int32, block.shape, axis) + tile_start(group)
    inside = (lane >= group * DK) & (lane < (group + 1) * DK)
    return jnp.where(inside, block, jnp.zeros_like(block))


def half_roll(block):
    return pltpu.roll(block, LANES // 2, block.ndim - 1)


def pack(block, group):
    first, second = block[..., :LANES], block[..., LANES:]
    even = group % 2 == 0
    full = jnp.where(even, first, second)
    half = jnp.where(even, second, first)
    rows = block.shape[1] // 2
    return full, half[:, :rows] + half_roll(half[:, rows:])


def unpack(full, folded, group):
    even = group % 2 == 0
    lane = lax.broadcasted_iota(jnp.int32, folded.shape, 2)
    inside = (lane < LANES // 2) == even
    low = jnp.where(inside, folded, 0.0)
    high = jnp.where(inside, half_roll(folded), 0.0)
    half = jnp.concatenate([low, high], axis=1)
    return jnp.where(even, full, half), jnp.where(even, half, full)


def dot(a, b, ca, cb):
    return lax.dot_general(a, b, (((ca,), (cb,)), ((), ())), preferred_element_type=jnp.float32)


def kernel(n_pb, n_ka, groups, own_heads, nq, rows, n_blocks, *refs):
    bits = n_pb.bit_length() - 1
    q_hbm, k_hbm, v_hbm, o_hbm, do_hbm, lse_hbm, vis_hbm = refs[:7]
    dq_ref, dk_ref, dv_ref = refs[7:10]
    (kv, own, qv, dov, ov, lse, vis, stat, dq_acc, dq_full, dq_s, dq_r, acc, whole_grad) = refs[10:24]
    rest = list(refs[24:])
    recvs = [rest.pop(0) for _ in range(bits)]
    sends = [None] + [rest.pop(0) for _ in range(bits - 1)]
    zs, zr, loc_sem, ag_s, ag_r, vs_s, vs_r, rs_s, rs_r, z_s, z_r, q_s, q_r = rest

    ka = lax.axis_index("ka")
    pb = lax.axis_index("pb")
    scale = DK ** (-0.5)
    width = 2 * LANES
    heads = own_heads * groups
    group = ka % groups
    first_head = (ka // groups) * heads
    hq = heads * nq
    k_start = pl.multiple_of(tile_start(group), LANES)
    v_start = pl.multiple_of(group * DV, LANES)
    head_part = pl.ds(first_head, heads)

    locals_ = [
        (k_hbm.at[:, pl.ds(k_start, width)], kv.at[ka, pb, :, pl.ds(0, width)]),
        (v_hbm.at[:, pl.ds(v_start, DV)], kv.at[ka, pb, :, pl.ds(width, DV)]),
    ]
    for g in range(groups):
        locals_ += [
            (k_hbm.at[:, pl.ds(tile_start(g), width)], own.at[g, :, pl.ds(0, width)]),
            (v_hbm.at[:, pl.ds(g * DV, DV)], own.at[g, :, pl.ds(width, DV)]),
        ]
    locals_ += [(vis_hbm, vis.at[ka])]
    first = len(locals_)
    locals_ += [
        (q_hbm.at[head_part, :, pl.ds(k_start, width)], qv),
        (do_hbm.at[head_part, :, pl.ds(v_start, DV)], dov),
        (o_hbm.at[head_part, :, pl.ds(v_start, DV)], ov),
        (lse_hbm, lse),
    ]
    loc = [pltpu.make_async_copy(a, b, loc_sem.at[i]) for i, (a, b) in enumerate(locals_)]
    for c in loc:
        c.start()

    barrier = pltpu.get_barrier_semaphore()
    for j in range(1, n_ka):
        pl.semaphore_signal(barrier, inc=1, device_id={"ka": flip(ka, j)}, device_id_type=MESH)
    for t in range(bits):
        pl.semaphore_signal(barrier, inc=1, device_id={"pb": flip(pb, 1 << t)}, device_id_type=MESH)
    for c in loc[:first]:
        c.wait()
    pl.semaphore_wait(barrier, n_ka - 1 + bits)

    pending = []

    def remote(src, dst, s_sem, r_sem, **peer):
        return pltpu.make_async_remote_copy(
            src_ref=src, dst_ref=dst, send_sem=s_sem, recv_sem=r_sem,
            device_id=peer, device_id_type=MESH,
        )

    def send(*args, **peer):
        copy = remote(*args, **peer)
        copy.start()
        pending.append(copy)

    def shard(j, m):
        return kv.at[flip(ka, j), flip(pb, m)]

    def wait_shard(j, m):
        peer = {"pb": flip(pb, low_bit(m))} if m else {"ka": flip(ka, j)}
        remote(shard(j, m), shard(j, m), ag_s.at[j, m], ag_r.at[j, m], **peer).wait_recv()

    def forward(j, m):
        bit = n_pb // 2
        while bit:
            if m == 0 or bit < low_bit(m):
                send(shard(j, m), shard(j, m), ag_s.at[j, m ^ bit], ag_r.at[j, m ^ bit], pb=flip(pb, bit))
            bit //= 2

    reached = {"z": 1, "x": 0}

    def relay_z(upto):
        while reached["z"] < min(upto, n_ka):
            wait_shard(reached["z"], 0)
            forward(reached["z"], 0)
            reached["z"] += 1

    def relay_x(upto):
        while reached["x"] < min(upto, n_ka):
            bit = n_pb // 2
            while bit > 1:
                for m in range(bit, n_pb, 2 * bit):
                    wait_shard(reached["x"], m)
                    forward(reached["x"], m)
                bit //= 2
            reached["x"] += 1

    for j in range(1, n_ka):
        far = flip(ka, j)
        send(own.at[far % groups], kv.at[ka, pb], ag_s.at[j, 0], ag_r.at[j, 0], ka=far)
    forward(0, 0)
    for j in range(1, n_ka):
        send(vis.at[ka], vis.at[ka], vs_s.at[j], vs_r.at[j], ka=flip(ka, j))

    for c in loc[first:]:
        c.wait()
    qv[...] = keep_group(qv[...], group)
    product = dov[...].astype(jnp.float32) * ov[...].astype(jnp.float32)
    stat[1:2, :] = jnp.sum(jnp.transpose(product.reshape(hq, DV)), axis=0, keepdims=True)
    for h in range(heads):
        stat[0:1, h * nq : (h + 1) * nq] = lse[group, pl.ds(first_head + h, 1), :]
    dq_acc[...] = jnp.zeros_like(dq_acc)

    per = min(n_pb, max(1, 256 // rows))
    chunk_rows = per * rows

    def compute_chunk(j, chunk):
        s = flip(ka, j)
        whole = kv[s, pl.ds(chunk * per, per)].reshape(chunk_rows, width + DV)
        if per == n_pb:
            seen = vis[s]
        else:
            seen = vis[s, :, pl.ds(pl.multiple_of(chunk * chunk_rows, chunk_rows), chunk_rows)]
        seen = seen.astype(jnp.float32)
        block = lax.broadcasted_iota(jnp.int32, (nq, chunk_rows), 0) // (nq // n_blocks)
        mask = jnp.zeros((nq, chunk_rows), jnp.float32)
        for b in range(n_blocks):
            mask = jnp.where(block == b, seen[b : b + 1, :], mask)
        mask = jnp.transpose(mask)
        mask = jnp.concatenate([mask] * heads, axis=1)
        keys = keep_group(whole[:, :width], group)
        values = whole[:, width:]
        grad = dov[...].reshape(hq, DV)
        query = qv[...].reshape(hq, width)
        scores = dot(keys, query, 1, 1) * scale
        probs = jnp.exp(scores - stat[0:1, :]) * mask
        grad_probs = dot(values, grad, 1, 1)
        grad_scores = (probs * (grad_probs - stat[1:2, :])).astype(jnp.bfloat16)
        value_grad = dot(probs.astype(jnp.bfloat16), grad, 1, 0)
        at = pl.ds(chunk * per, per)
        acc[j, at, 0:rows] = value_grad.reshape(per, rows, DV)
        key_grad = dot(grad_scores, query, 1, 0)
        full, folded = pack(key_grad.reshape(per, rows, width), group)
        acc[j, at, rows : 2 * rows] = full
        acc[j, at, 2 * rows :] = folded
        dq_acc[...] += dot(grad_scores, keys, 0, 0)

    def compute(j):
        for m in range(1, n_pb, 2):
            wait_shard(j, m)
        if j:
            s = flip(ka, j)
            remote(vis.at[s], vis.at[s], vs_s.at[j], vs_r.at[j], ka=s).wait_recv()
        if per == n_pb:
            compute_chunk(j, 0)
        else:
            lax.fori_loop(0, n_pb // per, lambda c, _: (compute_chunk(j, c), 0)[1], 0)
        for m in range(1, n_pb, 2):
            send(acc.at[j, flip(pb, m)], recvs[0].at[j, m >> 1], rs_s.at[j, m], rs_r.at[j, m], pb=flip(pb, 1))

    def reduce_stage(j, t):
        step = 2 << t
        for m in range(0, n_pb, step):
            slot = recvs[t].at[j, m >> (t + 1)]
            sem = m + (1 << t)
            remote(slot, slot, rs_s.at[j, sem], rs_r.at[j, sem], pb=flip(pb, 1 << t)).wait_recv()
            mine = flip(pb, m)
            total = acc[j, mine] + slot[...].astype(jnp.float32)
            if m & step:
                at = m >> (t + 2)
                sends[t + 1][j, at] = total.astype(jnp.bfloat16)
                send(
                    sends[t + 1].at[j, at], recvs[t + 1].at[j, at],
                    rs_s.at[j, m], rs_r.at[j, m], pb=flip(pb, step),
                )
            elif t == bits - 1 and j:
                zs[j] = total.astype(jnp.bfloat16)
                send(zs.at[j], zr.at[j], z_s.at[j], z_r.at[j], ka=flip(ka, j))
            else:
                acc[j, mine] = total

    def send_queries():
        for r in range(1, groups):
            far = flip(ka, r)
            part = dq_acc[pl.ds(pl.multiple_of((far % groups) * own_heads * nq, nq), own_heads * nq), :]
            full, folded = pack(part.reshape(own_heads, nq, width), group)
            dq_s[r, :, :nq] = full.astype(jnp.bfloat16)
            dq_s[r, :, nq:] = folded.astype(jnp.bfloat16)
            send(dq_s.at[r], dq_r.at[r], q_s.at[r], q_r.at[r], ka=far)
        mine = dq_acc[pl.ds(pl.multiple_of(group * own_heads * nq, nq), own_heads * nq), :]
        dq_full[group] = mine.reshape(own_heads, nq, width)

    relay_z(2)
    relay_x(1)
    for i in range(n_ka + bits):
        if i < n_ka:
            compute(i)
        relay_z(i + 4)
        relay_x(i + 2 if i == 0 else i + 3)
        if i == n_ka - 1:
            send_queries()
        for t in range(bits - 1, -1, -1):
            if 0 <= i - 1 - t < n_ka:
                reduce_stage(i - 1 - t, t)

    def join(pieces, columns):
        tiles = {}
        for g in range(groups):
            for c in range(2):
                at = tile_start(g) + c * LANES
                tile = pieces[g][c]
                tiles[at] = tiles[at] + tile if at in tiles else tile
        return [(at, tile) for at, tile in tiles.items() if at < columns]

    for r in range(1, groups):
        far = flip(ka, r)
        remote(dq_r.at[r], dq_r.at[r], q_s.at[r], q_r.at[r], ka=far).wait_recv()
        got = dq_r[r].astype(jnp.float32)
        left, right = unpack(got[:, :nq], got[:, nq:], far % groups)
        dq_full[far % groups, :, :, :LANES] = left
        dq_full[far % groups, :, :, LANES:] = right
    pieces = [(dq_full[g, :, :, :LANES], dq_full[g, :, :, LANES:]) for g in range(groups)]
    for at, tile in join(pieces, groups * DK):
        dq_ref[:, :, at : at + LANES] = tile * scale

    totals = [acc[0, pb]] + [None] * (groups - 1)
    for j in range(1, n_ka):
        remote(zr.at[j], zr.at[j], z_s.at[j], z_r.at[j], ka=flip(ka, j)).wait_recv()
        term = zr[j].astype(jnp.float32)
        r = j % groups
        totals[r] = term if totals[r] is None else totals[r] + term
    for r in range(groups):
        whole_grad[flip(group, r)] = totals[r]
    pieces = []
    for g in range(groups):
        dv_ref[:, g * DV : (g + 1) * DV] = whole_grad[g, 0:rows]
        left, right = unpack(
            whole_grad[g, rows : 2 * rows][None], whole_grad[g, 2 * rows :][None], jnp.int32(g)
        )
        pieces.append((left[0], right[0]))
    for at, tile in join(pieces, groups * DK):
        dk_ref[:, at : at + LANES] = tile * scale
    for copy in pending:
        copy.wait_send()


def per_device(n_pb, n_ka, queries, comp_keys, comp_values, outputs, grad_out, log_sums, visible):
    groups = comp_keys.shape[1] // DK
    all_heads, nq, _ = queries.shape
    heads = all_heads // n_ka
    rows = comp_keys.shape[0]
    bits = n_pb.bit_length() - 1
    n_blocks = visible.shape[0]
    f32, bf16 = jnp.float32, jnp.bfloat16
    width = 2 * LANES
    team = heads * groups
    packed = 2 * rows + rows // 2
    scratch = [
        pltpu.VMEM((n_ka, n_pb, rows, width + DV), bf16),
        pltpu.VMEM((groups, rows, width + DV), bf16),
        pltpu.VMEM((team, nq, width), bf16),
        pltpu.VMEM((team, nq, DV), bf16),
        pltpu.VMEM((team, nq, DV), bf16),
        pltpu.VMEM(log_sums.shape, f32),
        pltpu.VMEM((n_ka,) + visible.shape, jnp.int32),
        pltpu.VMEM((2, team * nq), f32),
        pltpu.VMEM((team * nq, width), f32),
        pltpu.VMEM((groups, heads, nq, width), f32),
        pltpu.VMEM((groups, heads, nq + nq // 2, LANES), bf16),
        pltpu.VMEM((groups, heads, nq + nq // 2, LANES), bf16),
        pltpu.VMEM((n_ka, n_pb, packed, LANES), f32),
        pltpu.VMEM((groups, packed, LANES), f32),
    ]
    scratch += [
        pltpu.VMEM((n_ka, n_pb >> (t + 1), packed, LANES), f32 if t == 0 else bf16)
        for t in range(bits)
    ]
    scratch += [pltpu.VMEM((n_ka, n_pb >> (t + 1), packed, LANES), bf16) for t in range(1, bits)]
    dma = pltpu.SemaphoreType.DMA
    scratch += [
        pltpu.VMEM((n_ka, packed, LANES), bf16),
        pltpu.VMEM((n_ka, packed, LANES), bf16),
        dma((7 + 2 * groups,)),
        dma((n_ka, n_pb)),
        dma((n_ka, n_pb)),
        dma((n_ka,)),
        dma((n_ka,)),
        dma((n_ka, n_pb)),
        dma((n_ka, n_pb)),
        dma((n_ka,)),
        dma((n_ka,)),
        dma((groups,)),
        dma((groups,)),
    ]
    return pl.pallas_call(
        functools.partial(kernel, n_pb, n_ka, groups, heads, nq, rows, n_blocks),
        out_shape=(
            pltpu.VMEM((heads, nq, queries.shape[2]), f32),
            pltpu.VMEM(comp_keys.shape, f32),
            pltpu.VMEM(comp_values.shape, f32),
        ),
        in_specs=[pl.BlockSpec(memory_space=pl.ANY)] * 7,
        out_specs=[pl.BlockSpec(memory_space=pltpu.VMEM)] * 3,
        scratch_shapes=scratch,
        compiler_params=pltpu.CompilerParams(
            collective_id=0, has_side_effects=True, vmem_limit_bytes=64000 * 1024
        ),
    )(queries, comp_keys, comp_values, outputs, grad_out, log_sums, visible)


def solution(mesh):
    n_pb, n_ka = mesh.shape["pb"], mesh.shape["ka"]
    return jax.shard_map(
        functools.partial(per_device, n_pb, n_ka),
        mesh=mesh,
        in_specs=(
            P(None, "pb", "ga"),
            P(("ka", "pb"), "ga"),
            P(("ka", "pb"), "ga"),
            P(None, "pb", "ga"),
            P(None, "pb", "ga"),
            P("ga", None, "pb"),
            P("pb", "ka"),
        ),
        out_specs=(P("ka", "pb", "ga"), P(("ka", "pb"), "ga"), P(("ka", "pb"), "ga")),
        check_vma=False,
    )
```

```python
import functools

import jax
import jax.numpy as jnp
from jax import lax
from jax.experimental import pallas as pl
from jax.experimental.pallas import tpu as pltpu
from jax.sharding import PartitionSpec as P

DK = 192
DV = 128
LANES = 128
MESH = pl.DeviceIdType.MESH


def flip(index, bits):
    bit = 1
    while bit <= bits:
        if bits & bit:
            index = index + bit - 2 * bit * ((index // bit) % 2)
        bit *= 2
    return index


def low_bit(m):
    return m & -m


def tile_start(group):
    return group * DK // LANES * LANES


def keep_group(block, group):
    axis = block.ndim - 1
    lane = lax.broadcasted_iota(jnp.int32, block.shape, axis) + tile_start(group)
    inside = (lane >= group * DK) & (lane < (group + 1) * DK)
    return jnp.where(inside, block, jnp.zeros_like(block))


def half_roll(block):
    return pltpu.roll(block, LANES // 2, block.ndim - 1)


def pack(block, group):
    first, second = block[..., :LANES], block[..., LANES:]
    even = group % 2 == 0
    full = jnp.where(even, first, second)
    half = jnp.where(even, second, first)
    rows = block.shape[1] // 2
    return full, half[:, :rows] + half_roll(half[:, rows:])


def unpack(full, folded, group):
    even = group % 2 == 0
    lane = lax.broadcasted_iota(jnp.int32, folded.shape, 2)
    inside = (lane < LANES // 2) == even
    low = jnp.where(inside, folded, 0.0)
    high = jnp.where(inside, half_roll(folded), 0.0)
    half = jnp.concatenate([low, high], axis=1)
    return jnp.where(even, full, half), jnp.where(even, half, full)


def dot(a, b, ca, cb):
    return lax.dot_general(a, b, (((ca,), (cb,)), ((), ())), preferred_element_type=jnp.float32)


def kernel(n_pb, n_ka, groups, own_heads, nq, rows, n_blocks, *refs):
    bits = n_pb.bit_length() - 1
    q_hbm, k_hbm, v_hbm, o_hbm, do_hbm, lse_hbm, vis_hbm = refs[:7]
    dq_ref, dk_ref, dv_ref = refs[7:10]
    (kv, own, qv, dov, ov, lse, vis, stat, dq_acc, dq_full, dq_s, dq_r, acc, whole_grad) = refs[10:24]
    rest = list(refs[24:])
    recvs = [rest.pop(0) for _ in range(bits)]
    sends = [None] + [rest.pop(0) for _ in range(bits - 1)]
    zs, zr, loc_sem, ag_s, ag_r, vs_s, vs_r, rs_s, rs_r, z_s, z_r, q_s, q_r = rest

    ka = lax.axis_index("ka")
    pb = lax.axis_index("pb")
    scale = DK ** (-0.5)
    width = 2 * LANES
    heads = own_heads * groups
    group = ka % groups
    first_head = (ka // groups) * heads
    hq = heads * nq
    k_start = pl.multiple_of(tile_start(group), LANES)
    v_start = pl.multiple_of(group * DV, LANES)
    head_part = pl.ds(first_head, heads)

    locals_ = [
        (k_hbm.at[:, pl.ds(k_start, width)], kv.at[ka, pb, :, pl.ds(0, width)]),
        (v_hbm.at[:, pl.ds(v_start, DV)], kv.at[ka, pb, :, pl.ds(width, DV)]),
    ]
    for g in range(groups):
        locals_ += [
            (k_hbm.at[:, pl.ds(tile_start(g), width)], own.at[g, :, pl.ds(0, width)]),
            (v_hbm.at[:, pl.ds(g * DV, DV)], own.at[g, :, pl.ds(width, DV)]),
        ]
    locals_ += [(vis_hbm, vis.at[ka])]
    first = len(locals_)
    locals_ += [
        (q_hbm.at[head_part, :, pl.ds(k_start, width)], qv),
        (do_hbm.at[head_part, :, pl.ds(v_start, DV)], dov),
        (o_hbm.at[head_part, :, pl.ds(v_start, DV)], ov),
        (lse_hbm, lse),
    ]
    loc = [pltpu.make_async_copy(a, b, loc_sem.at[i]) for i, (a, b) in enumerate(locals_)]
    for c in loc:
        c.start()

    barrier = pltpu.get_barrier_semaphore()
    for j in range(1, n_ka):
        pl.semaphore_signal(barrier, inc=1, device_id={"ka": flip(ka, j)}, device_id_type=MESH)
    for t in range(bits):
        pl.semaphore_signal(barrier, inc=1, device_id={"pb": flip(pb, 1 << t)}, device_id_type=MESH)
    for c in loc[:first]:
        c.wait()
    pl.semaphore_wait(barrier, n_ka - 1 + bits)

    pending = []

    def remote(src, dst, s_sem, r_sem, **peer):
        return pltpu.make_async_remote_copy(
            src_ref=src, dst_ref=dst, send_sem=s_sem, recv_sem=r_sem,
            device_id=peer, device_id_type=MESH,
        )

    def send(*args, **peer):
        copy = remote(*args, **peer)
        copy.start()
        pending.append(copy)

    def shard(j, m):
        return kv.at[flip(ka, j), flip(pb, m)]

    def wait_shard(j, m):
        peer = {"pb": flip(pb, low_bit(m))} if m else {"ka": flip(ka, j)}
        remote(shard(j, m), shard(j, m), ag_s.at[j, m], ag_r.at[j, m], **peer).wait_recv()

    def forward(j, m):
        bit = n_pb // 2
        while bit:
            if m == 0 or bit < low_bit(m):
                send(shard(j, m), shard(j, m), ag_s.at[j, m ^ bit], ag_r.at[j, m ^ bit], pb=flip(pb, bit))
            bit //= 2

    reached = {"z": 1, "x": 0}

    def relay_z(upto):
        while reached["z"] < min(upto, n_ka):
            wait_shard(reached["z"], 0)
            forward(reached["z"], 0)
            reached["z"] += 1

    def relay_x(upto):
        while reached["x"] < min(upto, n_ka):
            bit = n_pb // 2
            while bit > 1:
                for m in range(bit, n_pb, 2 * bit):
                    wait_shard(reached["x"], m)
                    forward(reached["x"], m)
                bit //= 2
            reached["x"] += 1

    for j in range(n_ka - 1, 0, -1):
        far = flip(ka, j)
        send(own.at[far % groups], kv.at[ka, pb], ag_s.at[j, 0], ag_r.at[j, 0], ka=far)
    forward(0, 0)
    for j in range(1, n_ka):
        send(vis.at[ka], vis.at[ka], vs_s.at[j], vs_r.at[j], ka=flip(ka, j))

    for c in loc[first:]:
        c.wait()
    qv[...] = keep_group(qv[...], group)
    product = dov[...].astype(jnp.float32) * ov[...].astype(jnp.float32)
    stat[1:2, :] = jnp.sum(jnp.transpose(product.reshape(hq, DV)), axis=0, keepdims=True)
    for h in range(heads):
        stat[0:1, h * nq : (h + 1) * nq] = lse[group, pl.ds(first_head + h, 1), :]
    dq_acc[...] = jnp.zeros_like(dq_acc)

    per = min(n_pb, max(1, 256 // rows))
    chunk_rows = per * rows

    def compute_chunk(j, chunk):
        s = flip(ka, j)
        whole = kv[s, pl.ds(chunk * per, per)].reshape(chunk_rows, width + DV)
        if per == n_pb:
            seen = vis[s]
        else:
            seen = vis[s, :, pl.ds(pl.multiple_of(chunk * chunk_rows, chunk_rows), chunk_rows)]
        seen = seen.astype(jnp.float32)
        block = lax.broadcasted_iota(jnp.int32, (nq, chunk_rows), 0) // (nq // n_blocks)
        mask = jnp.zeros((nq, chunk_rows), jnp.float32)
        for b in range(n_blocks):
            mask = jnp.where(block == b, seen[b : b + 1, :], mask)
        mask = jnp.transpose(mask)
        mask = jnp.concatenate([mask] * heads, axis=1)
        keys = keep_group(whole[:, :width], group)
        values = whole[:, width:]
        grad = dov[...].reshape(hq, DV)
        query = qv[...].reshape(hq, width)
        scores = dot(keys, query, 1, 1) * scale
        probs = jnp.exp(scores - stat[0:1, :]) * mask
        grad_probs = dot(values, grad, 1, 1)
        grad_scores = (probs * (grad_probs - stat[1:2, :])).astype(jnp.bfloat16)
        value_grad = dot(probs.astype(jnp.bfloat16), grad, 1, 0)
        at = pl.ds(chunk * per, per)
        acc[j, at, 0:rows] = value_grad.reshape(per, rows, DV)
        key_grad = dot(grad_scores, query, 1, 0)
        full, folded = pack(key_grad.reshape(per, rows, width), group)
        acc[j, at, rows : 2 * rows] = full
        acc[j, at, 2 * rows :] = folded
        dq_acc[...] += dot(grad_scores, keys, 0, 0)

    def compute(j):
        for m in range(1, n_pb, 2):
            wait_shard(j, m)
        if j:
            s = flip(ka, j)
            remote(vis.at[s], vis.at[s], vs_s.at[j], vs_r.at[j], ka=s).wait_recv()
        if per == n_pb:
            compute_chunk(j, 0)
        else:
            lax.fori_loop(0, n_pb // per, lambda c, _: (compute_chunk(j, c), 0)[1], 0)
        for m in range(1, n_pb, 2):
            send(acc.at[j, flip(pb, m)], recvs[0].at[j, m >> 1], rs_s.at[j, m], rs_r.at[j, m], pb=flip(pb, 1))

    def reduce_stage(j, t):
        step = 2 << t
        for m in range(0, n_pb, step):
            slot = recvs[t].at[j, m >> (t + 1)]
            sem = m + (1 << t)
            remote(slot, slot, rs_s.at[j, sem], rs_r.at[j, sem], pb=flip(pb, 1 << t)).wait_recv()
            mine = flip(pb, m)
            total = acc[j, mine] + slot[...].astype(jnp.float32)
            if m & step:
                at = m >> (t + 2)
                sends[t + 1][j, at] = total.astype(jnp.bfloat16)
                send(
                    sends[t + 1].at[j, at], recvs[t + 1].at[j, at],
                    rs_s.at[j, m], rs_r.at[j, m], pb=flip(pb, step),
                )
            elif t == bits - 1 and j:
                zs[j] = total.astype(jnp.bfloat16)
                send(zs.at[j], zr.at[j], z_s.at[j], z_r.at[j], ka=flip(ka, j))
            else:
                acc[j, mine] = total

    def send_queries():
        for r in range(1, groups):
            far = flip(ka, r)
            part = dq_acc[pl.ds(pl.multiple_of((far % groups) * own_heads * nq, nq), own_heads * nq), :]
            full, folded = pack(part.reshape(own_heads, nq, width), group)
            dq_s[r, :, :nq] = full.astype(jnp.bfloat16)
            dq_s[r, :, nq:] = folded.astype(jnp.bfloat16)
            send(dq_s.at[r], dq_r.at[r], q_s.at[r], q_r.at[r], ka=far)
        mine = dq_acc[pl.ds(pl.multiple_of(group * own_heads * nq, nq), own_heads * nq), :]
        dq_full[group] = mine.reshape(own_heads, nq, width)

    relay_z(2)
    relay_x(1)
    reduced = set()

    def reduce_once(j, t):
        if 0 <= j < n_ka and (j, t) not in reduced:
            reduced.add((j, t))
            reduce_stage(j, t)

    for i in range(n_ka + bits):
        if i < n_ka:
            compute(i)
        relay_z(i + 4)
        if i == 1:
            reduce_once(0, 0)
            reduce_once(1, 0)
        relay_x(i + 2 if i == 0 else i + 3)
        if i == n_ka - 1:
            send_queries()
        for t in range(bits):
            reduce_once(i - 1 - t, t)

    def join(pieces, columns):
        tiles = {}
        for g in range(groups):
            for c in range(2):
                at = tile_start(g) + c * LANES
                tile = pieces[g][c]
                tiles[at] = tiles[at] + tile if at in tiles else tile
        return [(at, tile) for at, tile in tiles.items() if at < columns]

    for r in range(1, groups):
        far = flip(ka, r)
        remote(dq_r.at[r], dq_r.at[r], q_s.at[r], q_r.at[r], ka=far).wait_recv()
        got = dq_r[r].astype(jnp.float32)
        left, right = unpack(got[:, :nq], got[:, nq:], far % groups)
        dq_full[far % groups, :, :, :LANES] = left
        dq_full[far % groups, :, :, LANES:] = right
    pieces = [(dq_full[g, :, :, :LANES], dq_full[g, :, :, LANES:]) for g in range(groups)]
    for at, tile in join(pieces, groups * DK):
        dq_ref[:, :, at : at + LANES] = tile * scale

    totals = [acc[0, pb]] + [None] * (groups - 1)
    for j in range(1, n_ka):
        remote(zr.at[j], zr.at[j], z_s.at[j], z_r.at[j], ka=flip(ka, j)).wait_recv()
        term = zr[j].astype(jnp.float32)
        r = j % groups
        totals[r] = term if totals[r] is None else totals[r] + term
    for r in range(groups):
        whole_grad[flip(group, r)] = totals[r]
    pieces = []
    for g in range(groups):
        dv_ref[:, g * DV : (g + 1) * DV] = whole_grad[g, 0:rows]
        left, right = unpack(
            whole_grad[g, rows : 2 * rows][None], whole_grad[g, 2 * rows :][None], jnp.int32(g)
        )
        pieces.append((left[0], right[0]))
    for at, tile in join(pieces, groups * DK):
        dk_ref[:, at : at + LANES] = tile * scale
    for copy in pending:
        copy.wait_send()


def per_device(n_pb, n_ka, queries, comp_keys, comp_values, outputs, grad_out, log_sums, visible):
    groups = comp_keys.shape[1] // DK
    all_heads, nq, _ = queries.shape
    heads = all_heads // n_ka
    rows = comp_keys.shape[0]
    bits = n_pb.bit_length() - 1
    n_blocks = visible.shape[0]
    f32, bf16 = jnp.float32, jnp.bfloat16
    width = 2 * LANES
    team = heads * groups
    packed = 2 * rows + rows // 2
    scratch = [
        pltpu.VMEM((n_ka, n_pb, rows, width + DV), bf16),
        pltpu.VMEM((groups, rows, width + DV), bf16),
        pltpu.VMEM((team, nq, width), bf16),
        pltpu.VMEM((team, nq, DV), bf16),
        pltpu.VMEM((team, nq, DV), bf16),
        pltpu.VMEM(log_sums.shape, f32),
        pltpu.VMEM((n_ka,) + visible.shape, jnp.int32),
        pltpu.VMEM((2, team * nq), f32),
        pltpu.VMEM((team * nq, width), f32),
        pltpu.VMEM((groups, heads, nq, width), f32),
        pltpu.VMEM((groups, heads, nq + nq // 2, LANES), bf16),
        pltpu.VMEM((groups, heads, nq + nq // 2, LANES), bf16),
        pltpu.VMEM((n_ka, n_pb, packed, LANES), f32),
        pltpu.VMEM((groups, packed, LANES), f32),
    ]
    scratch += [
        pltpu.VMEM((n_ka, n_pb >> (t + 1), packed, LANES), f32 if t == 0 else bf16)
        for t in range(bits)
    ]
    scratch += [pltpu.VMEM((n_ka, n_pb >> (t + 1), packed, LANES), bf16) for t in range(1, bits)]
    dma = pltpu.SemaphoreType.DMA
    scratch += [
        pltpu.VMEM((n_ka, packed, LANES), bf16),
        pltpu.VMEM((n_ka, packed, LANES), bf16),
        dma((7 + 2 * groups,)),
        dma((n_ka, n_pb)),
        dma((n_ka, n_pb)),
        dma((n_ka,)),
        dma((n_ka,)),
        dma((n_ka, n_pb)),
        dma((n_ka, n_pb)),
        dma((n_ka,)),
        dma((n_ka,)),
        dma((groups,)),
        dma((groups,)),
    ]
    return pl.pallas_call(
        functools.partial(kernel, n_pb, n_ka, groups, heads, nq, rows, n_blocks),
        out_shape=(
            pltpu.VMEM((heads, nq, queries.shape[2]), f32),
            pltpu.VMEM(comp_keys.shape, f32),
            pltpu.VMEM(comp_values.shape, f32),
        ),
        in_specs=[pl.BlockSpec(memory_space=pl.ANY)] * 7,
        out_specs=[pl.BlockSpec(memory_space=pltpu.VMEM)] * 3,
        scratch_shapes=scratch,
        compiler_params=pltpu.CompilerParams(
            collective_id=0, has_side_effects=True, vmem_limit_bytes=64000 * 1024
        ),
    )(queries, comp_keys, comp_values, outputs, grad_out, log_sums, visible)


def solution(mesh):
    n_pb, n_ka = mesh.shape["pb"], mesh.shape["ka"]
    return jax.shard_map(
        functools.partial(per_device, n_pb, n_ka),
        mesh=mesh,
        in_specs=(
            P(None, "pb", "ga"),
            P(("ka", "pb"), "ga"),
            P(("ka", "pb"), "ga"),
            P(None, "pb", "ga"),
            P(None, "pb", "ga"),
            P("ga", None, "pb"),
            P("pb", "ka"),
        ),
        out_specs=(P("ka", "pb", "ga"), P(("ka", "pb"), "ga"), P(("ka", "pb"), "ga")),
        check_vma=False,
    )
```
